32 devices in a mesh: groups: 2 (over y), blk: 4 (over z), uly: 2 (over x), cfg: 2 (over core).
Axes of the slice: x: 2, y: 2, z: 4, core: 2. Of those that a mesh axis runs over, the one named last changes fastest.
Arguments:
- query_rows: bfloat16 [2, 1024, 1536], P('cfg', ('groups', 'blk', 'uly')), parts along dimension 1, may hold values from -6 to 6
- key_rows: bfloat16 [2, 1024, 1536], P('cfg', ('groups', 'blk', 'uly')), parts along dimension 1, may hold values from -6 to 6
- value_rows: bfloat16 [2, 1024, 1536], P('cfg', ('groups', 'blk', 'uly')), parts along dimension 1, may hold values from -6 to 6
Outputs:
- attended: bfloat16 [2, 1024, 1536], P('cfg', ('groups', 'blk', 'uly')), parts along dimension 1
The draws below stay inside these ranges and needn't reach their ends.
There are 2 independent parts, one for each index of `groups`. The reference program is written for one: setup_inputs(seed, part) draws one part's arguments, and reference() takes and returns one part's arrays. A program takes and returns all parts, laid end to end along the dimension named above; each array names one. Nothing has to cross between parts.
All inputs are finite; a program needn't handle non-finite values.
Results may differ from the reference program's by a relative error of at most 0.0045.
Values may be sent and summed in bfloat16 or wider, within the bound.
A program may use at most 128 MiB of HBM per device.

```python
import math
import jax
import jax.numpy as jnp
from jax import lax

HEADS = 12
HD = 128
BRANCHES = 2
WIDTH = 1536
SEQ = 512


def joint_draw(key, which_one):
    shape = (BRANCHES, SEQ, WIDTH)
    own_key = jax.random.fold_in(key, 11 + which_one)
    base = jnp.clip(1.58 * jax.random.normal(own_key, shape, jnp.float32), -6.0, 6.0)
    return base.astype(jnp.bfloat16)


def draw_query_rows(key, part):
    return joint_draw(key, 0)


def draw_key_rows(key, part):
    return joint_draw(key, 1)


def shard_levels(rng, shape, split, low, top_value):
    loudness, own = 1.0, jax.random.fold_in(rng, 6)
    for axis_at, shards_of in split:
        heights = jnp.exp(jax.random.uniform(jax.random.fold_in(own, axis_at), (shards_of,), jnp.float32, low / len(split), top_value / len(split)))
        loudness = loudness * jnp.repeat(heights, shape[axis_at] // shards_of).reshape([-1 if axis == axis_at else 1 for axis in range(len(shape))])
    return loudness


def scatter_about(rng, shape, spread, most, shards=(), kind=jnp.bfloat16):
    loudness = shard_levels(rng, shape, shards, -0.22, 0.18) if shards else 1.0
    values = jax.random.normal(rng, shape, jnp.float32) * spread * loudness
    return jnp.minimum(jnp.maximum(values, -most), most).astype(kind)


def setup_inputs(seed: int = 0, part: int = 0) -> dict:
    arg_keys = jax.random.split(jax.random.key(seed), 4)
    part_splits = jax.random.split(jax.random.fold_in(arg_keys[3], part), 4)
    return {
        "query_rows": draw_query_rows(jax.random.fold_in(jax.random.fold_in(arg_keys[3], part), 71), part),
        "key_rows": draw_key_rows(jax.random.fold_in(jax.random.fold_in(arg_keys[3], part), 71), part),
        "value_rows": scatter_about(part_splits[2], (BRANCHES, SEQ, WIDTH), 1.0, 6.0, ((0, 2), (1, 8))),
    }


def one_head(triple):
    query_head, key_head, value_head = triple
    score_scale = 1.0 / math.sqrt(HD)
    scores = jnp.dot(query_head, key_head.T, preferred_element_type=jnp.float32) * score_scale
    row_max = lax.optimization_barrier(jnp.max(scores, axis=1, keepdims=True))
    weights = jnp.exp(scores - row_max)
    totals = lax.optimization_barrier(jnp.sum(weights, axis=1, keepdims=True))
    probabilities = weights.astype(jnp.bfloat16)
    mixed = jnp.dot(probabilities, value_head, preferred_element_type=jnp.float32)
    return (mixed / totals).astype(jnp.bfloat16)

def heads_first(array):
    return array.reshape(BRANCHES, SEQ, HEADS, HD).transpose(0, 2, 1, 3).reshape(BRANCHES * HEADS, SEQ, HD)

def reference(query_rows, key_rows, value_rows):
    result = lax.map(one_head, (heads_first(query_rows), heads_first(key_rows), heads_first(value_rows)))
    return result.reshape(BRANCHES, HEADS, SEQ, HD).transpose(0, 2, 1, 3).reshape(BRANCHES, SEQ, WIDTH)
```

```python
import functools
import math

import jax
import jax.numpy as jnp
from jax import lax
from jax.experimental import pallas as pl
from jax.experimental.pallas import tpu as pltpu
from jax.sharding import PartitionSpec as P

HD = 128
MESH = pl.DeviceIdType.MESH


def attend(queries, key_part, value_part):
    query_mat = queries[0, :, 0]
    row_count, head_count, head_size = query_mat.shape
    score_scale = 1.0 / math.sqrt(head_size)
    start_state = (
        jnp.full((head_count, row_count), -1e30, jnp.float32),
        jnp.zeros((head_count, row_count), jnp.float32),
        jnp.zeros((row_count, head_count, head_size), jnp.float32),
    )

    def absorb(state, pieces):
        key_piece = pieces[0][0, :, 0]
        value_piece = pieces[1][0, :, 0]
        scores = (
            jnp.einsum("qhd,khd->hqk", query_mat, key_piece, preferred_element_type=jnp.float32)
            * score_scale
        )
        running, totals, accumulated = state
        new_max = jnp.maximum(running, jnp.max(scores, axis=2))
        weights = jnp.exp(scores - new_max[:, :, None])
        factor = jnp.exp(running - new_max)
        totals = totals * factor + jnp.sum(weights, axis=2)
        probabilities = weights.astype(jnp.bfloat16)
        contrib = jnp.einsum(
            "hqk,khd->qhd", probabilities, value_piece, preferred_element_type=jnp.float32
        )
        accumulated = accumulated * factor.T[:, :, None] + contrib
        return (new_max, totals, accumulated)

    whole_keys, whole_values = (
        lax.all_gather(key_part, "blk", axis=1, tiled=True),
        lax.all_gather(value_part, "blk", axis=1, tiled=True),
    )
    key_count = whole_keys.shape[1]
    block_rows = math.gcd(key_count, 1024)

    def one_block(state, counter):
        offset = counter * block_rows
        key_block = lax.dynamic_slice_in_dim(whole_keys, offset, block_rows, 1)
        value_block = lax.dynamic_slice_in_dim(whole_values, offset, block_rows, 1)
        return (absorb(state, (key_block, value_block)), None)

    result, unused = lax.scan(
        one_block, start_state, jnp.arange(key_count // block_rows, dtype=jnp.int32)
    )
    output = (result[2] / result[1].T[:, :, None]).astype(jnp.bfloat16)
    return output.reshape(1, row_count, 1, head_count, head_size)


def gathered(query_rows, key_rows, value_rows):
    ulysses = lax.axis_size("uly")
    tokens = query_rows.shape[1]
    width = query_rows.shape[2]
    heads_local = width // HD // ulysses

    def moved(array):
        sections = array.reshape(1, tokens, ulysses, heads_local, HD)
        return lax.all_to_all(sections, "uly", split_axis=2, concat_axis=1, tiled=True)

    mixed = attend(moved(query_rows), moved(key_rows), moved(value_rows))
    merged = lax.all_to_all(mixed, "uly", split_axis=1, concat_axis=2, tiled=True)
    return merged.reshape(1, tokens, width)


def head_counts(heads_column, blocks):
    counts = [heads_column // blocks] * blocks
    by_middle = sorted(range(blocks), key=lambda z: (abs(2 * z - (blocks - 1)), z))
    for z in by_middle[: heads_column % blocks]:
        counts[z] += 1
    return counts


def exchange_kernel(
    blocks, ulys, rows, heads, q_ref, k_ref, v_ref, o_ref,
    qb, kb, vb, pb, ob, in_send, in_recv, out_send, out_recv,
):
    peers = blocks * ulys
    column = heads // ulys
    counts = head_counts(column, blocks)
    starts = [sum(counts[:z]) for z in range(blocks)]
    slots = max(counts)
    z = lax.axis_index("blk")
    x = lax.axis_index("uly")
    me = z * ulys + x
    sources = (q_ref, k_ref, v_ref)
    buffers = (qb, kb, vb)
    fold = (1.0 / math.sqrt(HD)) * math.log2(math.e)
    chunk_rows = ulys * rows

    def head_of(pz, px, s):
        return px * column + starts[pz] + s

    def owned(pz, px):
        return [head_of(pz, px, s) for s in range(counts[pz])]

    def piece(t, head):
        return sources[t].at[0, :, pl.ds(head * HD, HD)]

    def send_order(mz, mx):
        half = blocks // 2
        def rank(p):
            pz, px = p // ulys, p % ulys
            crosses = (pz < half) != (mz < half)
            return (not crosses, -abs(pz - mz), px == mx)
        return sorted((p for p in range(peers) if p != mz * ulys + mx), key=rank)

    def copies(mp):
        mz, mx = mp // ulys, mp % ulys
        made = []
        for s in range(slots):
            for group in ((0, 1), (2,)):
                for p in send_order(mz, mx):
                    pz, px = p // ulys, p % ulys
                    if s >= counts[pz]:
                        continue
                    for t in group:
                        made.append(
                            pltpu.make_async_remote_copy(
                                src_ref=piece(t, head_of(pz, px, s)),
                                dst_ref=buffers[t].at[s, pl.ds(mp * rows, rows)],
                                send_sem=in_send.at[s, t, p],
                                recv_sem=in_recv.at[s, t, mp],
                                device_id={"blk": pz, "uly": px},
                                device_id_type=MESH,
                            )
                        )
        return made

    barrier = pltpu.get_barrier_semaphore()
    for d in range(1, peers):
        peer = lax.rem(me + d, peers)
        pl.semaphore_signal(
            barrier, inc=1,
            device_id={"blk": peer // ulys, "uly": lax.rem(peer, ulys)},
            device_id_type=MESH,
        )
    for mp in range(peers):
        @pl.when(me == mp)
        def _():
            for s, head in enumerate(owned(mp // ulys, mp % ulys)):
                for t in range(3):
                    pltpu.make_async_copy(
                        piece(t, head), buffers[t].at[s, pl.ds(mp * rows, rows)],
                        in_recv.at[s, t, mp],
                    ).start()
    pl.semaphore_wait(barrier, peers - 1)

    for mp in range(peers):
        @pl.when(me == mp)
        def _():
            for copy in copies(mp):
                copy.start()

    first = jnp.int32(0)
    for i in range(blocks):
        first = first + jnp.where(z > i, counts[i], 0)
    my_head = x * column + first
    turn = jnp.where(z < blocks // 2, blocks // 2, 0)

    def landed(s, t):
        for p in range(peers):
            block = buffers[t].at[s, pl.ds(p * rows, rows)]
            pltpu.make_async_copy(block, block, in_recv.at[s, t, p]).wait()

    def out_copy(s, c, px):
        head = pl.multiple_of((my_head + s) * HD, HD)
        begin = pl.multiple_of((c * ulys + px) * rows, rows)
        return ob.at[s, pl.ds(begin, rows)], o_ref.at[0, :, pl.ds(head, HD)]

    def out_remote(s, c, px):
        src, dst = out_copy(s, c, px)
        return pltpu.make_async_remote_copy(
            src_ref=src, dst_ref=dst,
            send_sem=out_send.at[s, c * ulys + px],
            recv_sem=out_recv.at[my_head + s],
            device_id={"blk": c, "uly": px}, device_id_type=MESH,
        )

    def out_local(s, c, px):
        src, dst = out_copy(s, c, px)
        return pltpu.make_async_copy(src, dst, out_recv.at[my_head + s])

    def one_slot(s):
        landed(s, 0)
        landed(s, 1)
        totals = []
        for i in range(blocks):
            c = lax.rem(turn + i, blocks)
            span = pl.ds(pl.multiple_of(c * chunk_rows, chunk_rows), chunk_rows)
            scores = lax.dot_general(
                qb[s, span, :], kb[s], (((1,), (1,)), ((), ())),
                preferred_element_type=jnp.float32,
            )
            top = jnp.max(scores, axis=1, keepdims=True)
            weights = jnp.exp2((scores - top) * fold)
            totals.append(jnp.sum(weights, axis=1, keepdims=True))
            pb[span, :] = weights.astype(jnp.bfloat16)
        landed(s, 2)
        for i in range(blocks):
            c = lax.rem(turn + i, blocks)
            span = pl.ds(pl.multiple_of(c * chunk_rows, chunk_rows), chunk_rows)
            mixed = jnp.dot(pb[span, :], vb[s], preferred_element_type=jnp.float32)
            ob[s, span, :] = (mixed / totals[i]).astype(jnp.bfloat16)
            for px in range(ulys):
                mine = jnp.logical_and(c == z, x == px)

                @pl.when(mine)
                def _():
                    out_local(s, c, px).start()

                @pl.when(jnp.logical_not(mine))
                def _():
                    out_remote(s, c, px).start()

    def holds(s):
        has = z < 0
        for i in range(blocks):
            if counts[i] > s:
                has = jnp.logical_or(has, z == i)
        return has

    for s in range(slots):
        if min(counts) > s:
            one_slot(s)
        else:
            pl.when(holds(s))(functools.partial(one_slot, s))

    for head in range(heads):
        block = o_ref.at[0, :, pl.ds(head * HD, HD)]
        pltpu.make_async_copy(block, block, out_recv.at[head]).wait()

    for mp in range(peers):
        @pl.when(me == mp)
        def _():
            mz, mx = mp // ulys, mp % ulys
            for copy in copies(mp):
                copy.wait_send()
            for s in range(counts[mz]):
                for p in range(peers):
                    if p != mp:
                        out_remote(s, p // ulys, p % ulys).wait_send()


def exchanged(query_rows, key_rows, value_rows):
    blocks = lax.axis_size("blk")
    ulys = lax.axis_size("uly")
    unused, rows, width = query_rows.shape
    heads = width // HD
    peers = blocks * ulys
    slots = max(head_counts(heads // ulys, blocks))
    total = peers * rows
    return pl.pallas_call(
        functools.partial(exchange_kernel, blocks, ulys, rows, heads),
        out_shape=jax.ShapeDtypeStruct(query_rows.shape, jnp.bfloat16),
        in_specs=[pl.BlockSpec(memory_space=pl.ANY)] * 3,
        out_specs=pl.BlockSpec(memory_space=pl.ANY),
        scratch_shapes=[
            pltpu.VMEM((slots, total, HD), jnp.bfloat16),
            pltpu.VMEM((slots, total, HD), jnp.bfloat16),
            pltpu.VMEM((slots, total, HD), jnp.bfloat16),
            pltpu.VMEM((total, total), jnp.bfloat16),
            pltpu.VMEM((slots, total, HD), jnp.bfloat16),
            pltpu.SemaphoreType.DMA((slots, 3, peers)),
            pltpu.SemaphoreType.DMA((slots, 3, peers)),
            pltpu.SemaphoreType.DMA((slots, peers)),
            pltpu.SemaphoreType.DMA((heads,)),
        ],
        compiler_params=pltpu.CompilerParams(collective_id=0, has_side_effects=True),
    )(query_rows, key_rows, value_rows)


def local(query_rows, key_rows, value_rows):
    blocks = lax.axis_size("blk")
    ulys = lax.axis_size("uly")
    heads = query_rows.shape[2] // HD
    tokens = query_rows.shape[1] * blocks * ulys
    if heads % ulys == 0 and heads // ulys >= blocks and tokens <= 1024:
        return exchanged(query_rows, key_rows, value_rows)
    return gathered(query_rows, key_rows, value_rows)


def solution(mesh):
    spec = P("cfg", ("groups", "blk", "uly"), None)
    return jax.shard_map(
        local, mesh=mesh, in_specs=(spec, spec, spec), out_specs=spec, check_vma=False
    )
```

```python
import functools
import math

import jax
import jax.numpy as jnp
from jax import lax
from jax.experimental import pallas as pl
from jax.experimental.pallas import tpu as pltpu
from jax.sharding import PartitionSpec as P

HD = 128
MESH = pl.DeviceIdType.MESH


def attend(queries, key_part, value_part):
    query_mat = queries[0, :, 0]
    row_count, head_count, head_size = query_mat.shape
    score_scale = 1.0 / math.sqrt(head_size)
    start_state = (
        jnp.full((head_count, row_count), -1e30, jnp.float32),
        jnp.zeros((head_count, row_count), jnp.float32),
        jnp.zeros((row_count, head_count, head_size), jnp.float32),
    )

    def absorb(state, pieces):
        key_piece = pieces[0][0, :, 0]
        value_piece = pieces[1][0, :, 0]
        scores = (
            jnp.einsum("qhd,khd->hqk", query_mat, key_piece, preferred_element_type=jnp.float32)
            * score_scale
        )
        running, totals, accumulated = state
        new_max = jnp.maximum(running, jnp.max(scores, axis=2))
        weights = jnp.exp(scores - new_max[:, :, None])
        factor = jnp.exp(running - new_max)
        totals = totals * factor + jnp.sum(weights, axis=2)
        probabilities = weights.astype(jnp.bfloat16)
        contrib = jnp.einsum(
            "hqk,khd->qhd", probabilities, value_piece, preferred_element_type=jnp.float32
        )
        accumulated = accumulated * factor.T[:, :, None] + contrib
        return (new_max, totals, accumulated)

    whole_keys, whole_values = (
        lax.all_gather(key_part, "blk", axis=1, tiled=True),
        lax.all_gather(value_part, "blk", axis=1, tiled=True),
    )
    key_count = whole_keys.shape[1]
    block_rows = math.gcd(key_count, 1024)

    def one_block(state, counter):
        offset = counter * block_rows
        key_block = lax.dynamic_slice_in_dim(whole_keys, offset, block_rows, 1)
        value_block = lax.dynamic_slice_in_dim(whole_values, offset, block_rows, 1)
        return (absorb(state, (key_block, value_block)), None)

    result, unused = lax.scan(
        one_block, start_state, jnp.arange(key_count // block_rows, dtype=jnp.int32)
    )
    output = (result[2] / result[1].T[:, :, None]).astype(jnp.bfloat16)
    return output.reshape(1, row_count, 1, head_count, head_size)


def gathered(query_rows, key_rows, value_rows):
    ulysses = lax.axis_size("uly")
    tokens = query_rows.shape[1]
    width = query_rows.shape[2]
    heads_local = width // HD // ulysses

    def moved(array):
        sections = array.reshape(1, tokens, ulysses, heads_local, HD)
        return lax.all_to_all(sections, "uly", split_axis=2, concat_axis=1, tiled=True)

    mixed = attend(moved(query_rows), moved(key_rows), moved(value_rows))
    merged = lax.all_to_all(mixed, "uly", split_axis=1, concat_axis=2, tiled=True)
    return merged.reshape(1, tokens, width)


def head_counts(heads_column, blocks):
    counts = [heads_column // blocks] * blocks
    by_middle = sorted(range(blocks), key=lambda z: (abs(2 * z - (blocks - 1)), z))
    for z in by_middle[: heads_column % blocks]:
        counts[z] += 1
    return counts


def exchange_kernel(
    blocks, ulys, rows, heads, q_ref, k_ref, v_ref, o_ref,
    qb, kb, vb, pb, ob, in_send, in_recv, out_send, out_recv, row_in,
):
    peers = blocks * ulys
    column = heads // ulys
    counts = head_counts(column, blocks)
    starts = [sum(counts[:z]) for z in range(blocks)]
    slots = max(counts)
    z = lax.axis_index("blk")
    x = lax.axis_index("uly")
    me = z * ulys + x
    sources = (q_ref, k_ref, v_ref)
    buffers = (qb, kb, vb)
    fold = (1.0 / math.sqrt(HD)) * math.log2(math.e)
    chunk_rows = ulys * rows

    def head_of(pz, px, s):
        return px * column + starts[pz] + s

    def owned(pz, px):
        return [head_of(pz, px, s) for s in range(counts[pz])]

    def piece(t, head):
        return sources[t].at[0, :, pl.ds(head * HD, HD)]

    def half_of(pz):
        return 2 * pz >= blocks

    def copy_to(mp, s, t, p):
        pz, px = p // ulys, p % ulys
        return pltpu.make_async_remote_copy(
            src_ref=piece(t, head_of(pz, px, s)),
            dst_ref=buffers[t].at[s, pl.ds(mp * rows, rows)],
            send_sem=in_send.at[s, t, p],
            recv_sem=in_recv.at[s, t, mp],
            device_id={"blk": pz, "uly": px},
            device_id_type=MESH,
        )

    def later_order(mz, mx):
        others = [p for p in range(peers) if p != mz * ulys + mx]
        return sorted(
            others,
            key=lambda p: (half_of(p // ulys) == half_of(mz), abs(p // ulys - mz), p % ulys != mx),
        )

    def token(row, mz, mx, to):
        pl.semaphore_signal(
            row_in.at[row], inc=1, device_id={"blk": to, "uly": mx}, device_id_type=MESH
        )

    def send_inputs(mp):
        mz, mx = mp // ulys, mp % ulys
        inside = lambda pz: 0 <= pz < blocks

        def early(targets):
            for p in targets:
                for t in range(3):
                    copy_to(mp, 0, t, p).start()

        sides = (mz - 1, mz + 1) if half_of(mz) else (mz + 1, mz - 1)
        for pz in sides:
            if inside(pz):
                token(mz, mz, mx, pz)
        early([pz * ulys + mx for pz in sides if inside(pz)])
        early([mz * ulys + px for px in range(ulys) if px != mx])
        for d in range(1, blocks):
            for step in (mz - d, mz + d) if half_of(mz) else (mz + d, mz - d):
                if not inside(step):
                    continue
                pl.semaphore_wait(row_in.at[step], 1)
                onward = mz + 1 if step < mz else mz - 1
                if inside(onward):
                    token(step, mz, mx, onward)
                early([step * ulys + px for px in range(ulys) if d > 1 or px != mx])
        for s in range(1, slots):
            for group in ((0, 1), (2,)):
                for p in later_order(mz, mx):
                    if s < counts[p // ulys]:
                        for t in group:
                            copy_to(mp, s, t, p).start()

    barrier = pltpu.get_barrier_semaphore()

    def greet(pz, px):
        pl.semaphore_signal(
            barrier, inc=1, device_id={"blk": pz, "uly": px}, device_id_type=MESH
        )

    pl.when(z > 0)(lambda: greet(z - 1, x))
    pl.when(z < blocks - 1)(lambda: greet(z + 1, x))
    for d in range(1, ulys):
        greet(z, lax.rem(x + d, ulys))
    for mp in range(peers):
        @pl.when(me == mp)
        def _():
            for s, head in enumerate(owned(mp // ulys, mp % ulys)):
                for t in range(3):
                    pltpu.make_async_copy(
                        piece(t, head), buffers[t].at[s, pl.ds(mp * rows, rows)],
                        in_recv.at[s, t, mp],
                    ).start()
    greeted = (ulys - 1) + jnp.where(z > 0, 1, 0) + jnp.where(z < blocks - 1, 1, 0)
    pl.semaphore_wait(barrier, greeted)

    for mp in range(peers):
        @pl.when(me == mp)
        def _():
            send_inputs(mp)

    first = jnp.int32(0)
    for i in range(blocks):
        first = first + jnp.where(z > i, counts[i], 0)
    my_head = x * column + first
    turn = jnp.where(z < blocks // 2, blocks // 2, 0)

    def landed(s, t):
        for p in range(peers):
            block = buffers[t].at[s, pl.ds(p * rows, rows)]
            pltpu.make_async_copy(block, block, in_recv.at[s, t, p]).wait()

    def out_copy(s, c, px):
        head = pl.multiple_of((my_head + s) * HD, HD)
        begin = pl.multiple_of((c * ulys + px) * rows, rows)
        return ob.at[s, pl.ds(begin, rows)], o_ref.at[0, :, pl.ds(head, HD)]

    def out_remote(s, c, px):
        src, dst = out_copy(s, c, px)
        return pltpu.make_async_remote_copy(
            src_ref=src, dst_ref=dst,
            send_sem=out_send.at[s, c * ulys + px],
            recv_sem=out_recv.at[my_head + s],
            device_id={"blk": c, "uly": px}, device_id_type=MESH,
        )

    def out_local(s, c, px):
        src, dst = out_copy(s, c, px)
        return pltpu.make_async_copy(src, dst, out_recv.at[my_head + s])

    def one_slot(s):
        landed(s, 0)
        landed(s, 1)
        totals = []
        for i in range(blocks):
            c = lax.rem(turn + i, blocks)
            span = pl.ds(pl.multiple_of(c * chunk_rows, chunk_rows), chunk_rows)
            scores = lax.dot_general(
                qb[s, span, :], kb[s], (((1,), (1,)), ((), ())),
                preferred_element_type=jnp.float32,
            )
            top = jnp.max(scores, axis=1, keepdims=True)
            weights = jnp.exp2((scores - top) * fold)
            totals.append(jnp.sum(weights, axis=1, keepdims=True))
            pb[span, :] = weights.astype(jnp.bfloat16)
        landed(s, 2)
        for i in range(blocks):
            c = lax.rem(turn + i, blocks)
            span = pl.ds(pl.multiple_of(c * chunk_rows, chunk_rows), chunk_rows)
            mixed = jnp.dot(pb[span, :], vb[s], preferred_element_type=jnp.float32)
            ob[s, span, :] = (mixed / totals[i]).astype(jnp.bfloat16)
            for px in range(ulys):
                mine = jnp.logical_and(c == z, x == px)

                @pl.when(mine)
                def _():
                    out_local(s, c, px).start()

                @pl.when(jnp.logical_not(mine))
                def _():
                    out_remote(s, c, px).start()

    def holds(s):
        has = z < 0
        for i in range(blocks):
            if counts[i] > s:
                has = jnp.logical_or(has, z == i)
        return has

    for s in range(slots):
        if min(counts) > s:
            one_slot(s)
        else:
            pl.when(holds(s))(functools.partial(one_slot, s))

    for head in range(heads):
        block = o_ref.at[0, :, pl.ds(head * HD, HD)]
        pltpu.make_async_copy(block, block, out_recv.at[head]).wait()

    for mp in range(peers):
        @pl.when(me == mp)
        def _():
            mz, mx = mp // ulys, mp % ulys
            for p in range(peers):
                for s in range(counts[p // ulys]):
                    for t in range(3):
                        if p != mp:
                            copy_to(mp, s, t, p).wait_send()
            for s in range(counts[mz]):
                for p in range(peers):
                    if p != mp:
                        out_remote(s, p // ulys, p % ulys).wait_send()


def exchanged(query_rows, key_rows, value_rows):
    blocks = lax.axis_size("blk")
    ulys = lax.axis_size("uly")
    unused, rows, width = query_rows.shape
    heads = width // HD
    peers = blocks * ulys
    slots = max(head_counts(heads // ulys, blocks))
    total = peers * rows
    return pl.pallas_call(
        functools.partial(exchange_kernel, blocks, ulys, rows, heads),
        out_shape=pltpu.VMEM(query_rows.shape, jnp.bfloat16),
        in_specs=[pl.BlockSpec(memory_space=pl.ANY)] * 3,
        out_specs=pl.BlockSpec(memory_space=pltpu.VMEM),
        scratch_shapes=[
            pltpu.VMEM((slots, total, HD), jnp.bfloat16),
            pltpu.VMEM((slots, total, HD), jnp.bfloat16),
            pltpu.VMEM((slots, total, HD), jnp.bfloat16),
            pltpu.VMEM((total, total), jnp.bfloat16),
            pltpu.VMEM((slots, total, HD), jnp.bfloat16),
            pltpu.SemaphoreType.DMA((slots, 3, peers)),
            pltpu.SemaphoreType.DMA((slots, 3, peers)),
            pltpu.SemaphoreType.DMA((slots, peers)),
            pltpu.SemaphoreType.DMA((heads,)),
            pltpu.SemaphoreType.REGULAR((blocks,)),
        ],
        compiler_params=pltpu.CompilerParams(collective_id=0, has_side_effects=True),
    )(query_rows, key_rows, value_rows)


def local(query_rows, key_rows, value_rows):
    blocks = lax.axis_size("blk")
    ulys = lax.axis_size("uly")
    heads = query_rows.shape[2] // HD
    tokens = query_rows.shape[1] * blocks * ulys
    if heads % ulys == 0 and heads // ulys >= blocks and tokens <= 1024:
        return exchanged(query_rows, key_rows, value_rows)
    return gathered(query_rows, key_rows, value_rows)


def solution(mesh):
    spec = P("cfg", ("groups", "blk", "uly"), None)
    return jax.shard_map(
        local, mesh=mesh, in_specs=(spec, spec, spec), out_specs=spec, check_vma=False
    )
```

```python
import functools
import math

import jax
import jax.numpy as jnp
from jax import lax
from jax.experimental import pallas as pl
from jax.experimental.pallas import tpu as pltpu
from jax.sharding import PartitionSpec as P

HD = 128
MESH = pl.DeviceIdType.MESH


def attend(queries, key_part, value_part):
    query_mat = queries[0, :, 0]
    row_count, head_count, head_size = query_mat.shape
    score_scale = 1.0 / math.sqrt(head_size)
    start_state = (
        jnp.full((head_count, row_count), -1e30, jnp.float32),
        jnp.zeros((head_count, row_count), jnp.float32),
        jnp.zeros((row_count, head_count, head_size), jnp.float32),
    )

    def absorb(state, pieces):
        key_piece = pieces[0][0, :, 0]
        value_piece = pieces[1][0, :, 0]
        scores = (
            jnp.einsum("qhd,khd->hqk", query_mat, key_piece, preferred_element_type=jnp.float32)
            * score_scale
        )
        running, totals, accumulated = state
        new_max = jnp.maximum(running, jnp.max(scores, axis=2))
        weights = jnp.exp(scores - new_max[:, :, None])
        factor = jnp.exp(running - new_max)
        totals = totals * factor + jnp.sum(weights, axis=2)
        probabilities = weights.astype(jnp.bfloat16)
        contrib = jnp.einsum(
            "hqk,khd->qhd", probabilities, value_piece, preferred_element_type=jnp.float32
        )
        accumulated = accumulated * factor.T[:, :, None] + contrib
        return (new_max, totals, accumulated)

    whole_keys, whole_values = (
        lax.all_gather(key_part, "blk", axis=1, tiled=True),
        lax.all_gather(value_part, "blk", axis=1, tiled=True),
    )
    key_count = whole_keys.shape[1]
    block_rows = math.gcd(key_count, 1024)

    def one_block(state, counter):
        offset = counter * block_rows
        key_block = lax.dynamic_slice_in_dim(whole_keys, offset, block_rows, 1)
        value_block = lax.dynamic_slice_in_dim(whole_values, offset, block_rows, 1)
        return (absorb(state, (key_block, value_block)), None)

    result, unused = lax.scan(
        one_block, start_state, jnp.arange(key_count // block_rows, dtype=jnp.int32)
    )
    output = (result[2] / result[1].T[:, :, None]).astype(jnp.bfloat16)
    return output.reshape(1, row_count, 1, head_count, head_size)


def gathered(query_rows, key_rows, value_rows):
    ulysses = lax.axis_size("uly")
    tokens = query_rows.shape[1]
    width = query_rows.shape[2]
    heads_local = width // HD // ulysses

    def moved(array):
        sections = array.reshape(1, tokens, ulysses, heads_local, HD)
        return lax.all_to_all(sections, "uly", split_axis=2, concat_axis=1, tiled=True)

    mixed = attend(moved(query_rows), moved(key_rows), moved(value_rows))
    merged = lax.all_to_all(mixed, "uly", split_axis=1, concat_axis=2, tiled=True)
    return merged.reshape(1, tokens, width)


def head_counts(heads_column, blocks):
    counts = [heads_column // blocks] * blocks
    by_middle = sorted(range(blocks), key=lambda z: (abs(2 * z - (blocks - 1)), z))
    for z in by_middle[: heads_column % blocks]:
        counts[z] += 1
    return counts


def exchange_kernel(
    blocks, ulys, rows, heads, q_ref, k_ref, v_ref, o_ref,
    qb, kb, vb, pb, ob, in_send, in_recv, out_send, out_recv, row_in,
):
    peers = blocks * ulys
    column = heads // ulys
    counts = head_counts(column, blocks)
    starts = [sum(counts[:z]) for z in range(blocks)]
    slots = max(counts)
    z = lax.axis_index("blk")
    x = lax.axis_index("uly")
    me = z * ulys + x
    sources = (q_ref, k_ref, v_ref)
    buffers = (qb, kb, vb)
    fold = (1.0 / math.sqrt(HD)) * math.log2(math.e)
    chunk_rows = ulys * rows

    def first_of(pz):
        first = jnp.int32(0)
        for i in range(blocks):
            first = first + jnp.where(pz > i, counts[i], 0)
        return first

    def holds_at(pz, s):
        has = pz < 0
        for i in range(blocks):
            if counts[i] > s:
                has = jnp.logical_or(has, pz == i)
        return has

    my_head = x * column + first_of(z)
    my_rows = pl.ds(pl.multiple_of(me * rows, rows), rows)
    turn = jnp.where(z < blocks // 2, blocks // 2, 0)

    def piece(t, head):
        return sources[t].at[0, :, pl.ds(pl.multiple_of(head * HD, HD), HD)]

    def copy_to(s, t, pz, px):
        return pltpu.make_async_remote_copy(
            src_ref=piece(t, px * column + first_of(pz) + s),
            dst_ref=buffers[t].at[s, my_rows],
            send_sem=in_send.at[s, t, pz * ulys + px],
            recv_sem=in_recv.at[s, t, me],
            device_id={"blk": pz, "uly": px},
            device_id_type=MESH,
        )

    def send(s, pz, px):
        for t in range(3):
            copy_to(s, t, pz, px).start()

    def token(row, to):
        pl.semaphore_signal(
            row_in.at[row], inc=1, device_id={"blk": to, "uly": x}, device_id_type=MESH
        )

    toward = jnp.where(z < blocks // 2, 1, -1)

    def inside(pz):
        return jnp.logical_and(pz >= 0, pz < blocks)

    def send_inputs():
        def adjacent(side):
            pz = z + side

            @pl.when(inside(pz))
            def _():
                token(z, pz)
                send(0, pz, x)

        adjacent(toward)
        adjacent(-toward)
        for d in range(1, ulys):
            send(0, z, lax.rem(x + d, ulys))

        def further(d, side):
            pz = z + side * d
            onward = z - side

            @pl.when(inside(pz))
            def _():
                pl.semaphore_wait(row_in.at[pz], 1)
                pl.when(inside(onward))(lambda: token(pz, onward))
                for e in range(1, ulys):
                    send(0, pz, lax.rem(x + e, ulys))
                if d > 1:
                    send(0, pz, x)

        for d in range(1, blocks):
            further(d, toward)
            further(d, -toward)
        for s in range(1, slots):
            for i in range(blocks):
                pz = lax.rem(turn + i, blocks)
                for e in range(ulys):
                    px = lax.rem(x + e, ulys)
                    other = jnp.logical_or(pz != z, px != x)
                    pl.when(jnp.logical_and(holds_at(pz, s), other))(
                        functools.partial(send, s, pz, px)
                    )

    barrier = pltpu.get_barrier_semaphore()

    def greet(pz, px):
        pl.semaphore_signal(
            barrier, inc=1, device_id={"blk": pz, "uly": px}, device_id_type=MESH
        )

    pl.when(z > 0)(lambda: greet(z - 1, x))
    pl.when(z < blocks - 1)(lambda: greet(z + 1, x))
    for d in range(1, ulys):
        greet(z, lax.rem(x + d, ulys))
    def own(s):
        for t in range(3):
            pltpu.make_async_copy(
                piece(t, my_head + s), buffers[t].at[s, my_rows], in_recv.at[s, t, me]
            ).start()

    for s in range(slots):
        pl.when(holds_at(z, s))(functools.partial(own, s))
    greeted = (ulys - 1) + jnp.where(z > 0, 1, 0) + jnp.where(z < blocks - 1, 1, 0)
    pl.semaphore_wait(barrier, greeted)

    send_inputs()

    def landed(s, t):
        def one(p, carry):
            block = buffers[t].at[s, pl.ds(pl.multiple_of(p * rows, rows), rows)]
            pltpu.make_async_copy(block, block, in_recv.at[s, t, p]).wait()
            return carry

        lax.fori_loop(0, peers, one, 0)

    def out_copy(s, c, px):
        head = pl.multiple_of((my_head + s) * HD, HD)
        begin = pl.multiple_of((c * ulys + px) * rows, rows)
        return ob.at[s, pl.ds(begin, rows)], o_ref.at[0, :, pl.ds(head, HD)]

    def out_remote(s, c, px):
        src, dst = out_copy(s, c, px)
        return pltpu.make_async_remote_copy(
            src_ref=src, dst_ref=dst,
            send_sem=out_send.at[s, c * ulys + px],
            recv_sem=out_recv.at[my_head + s],
            device_id={"blk": c, "uly": px}, device_id_type=MESH,
        )

    def out_local(s, c, px):
        src, dst = out_copy(s, c, px)
        return pltpu.make_async_copy(src, dst, out_recv.at[my_head + s])

    late = jnp.logical_and(lax.axis_index("cfg") == 1, holds_at(z, slots - 1))

    def send_output(s, c):
        for px in range(ulys):
            mine = jnp.logical_and(c == z, x == px)

            @pl.when(mine)
            def _():
                out_local(s, c, px).start()

            @pl.when(jnp.logical_not(mine))
            def _():
                out_remote(s, c, px).start()

    def send_late():
        for s in range(slots - 1):
            for i in range((blocks + 1) // 2):
                send_output(s, jnp.where(z < blocks // 2, blocks - 1 - i, i))

    def one_slot(s):
        landed(s, 0)
        landed(s, 1)
        totals = []
        for i in range(blocks):
            c = jnp.where(z < blocks // 2, blocks - 1 - i, i)
            span = pl.ds(pl.multiple_of(c * chunk_rows, chunk_rows), chunk_rows)
            scores = lax.dot_general(
                qb[s, span, :], kb[s], (((1,), (1,)), ((), ())),
                preferred_element_type=jnp.float32,
            )
            top = jnp.max(scores, axis=1, keepdims=True)
            weights = jnp.exp2((scores - top) * fold)
            totals.append(jnp.sum(weights, axis=1, keepdims=True))
            pb[span, :] = weights.astype(jnp.bfloat16)
        landed(s, 2)
        if s > 0 and s == slots - 1:
            pl.when(late)(send_late)
        for i in range(blocks):
            c = jnp.where(z < blocks // 2, blocks - 1 - i, i)
            span = pl.ds(pl.multiple_of(c * chunk_rows, chunk_rows), chunk_rows)
            mixed = jnp.dot(pb[span, :], vb[s], preferred_element_type=jnp.float32)
            ob[s, span, :] = (mixed / totals[i]).astype(jnp.bfloat16)
            if s < slots - 1 and 2 * i < blocks:
                pl.when(jnp.logical_not(late))(functools.partial(send_output, s, c))
            else:
                send_output(s, c)

    for s in range(slots):
        if min(counts) > s:
            one_slot(s)
        else:
            pl.when(holds_at(z, s))(functools.partial(one_slot, s))

    def result_landed(head, carry):
        block = o_ref.at[0, :, pl.ds(pl.multiple_of(head * HD, HD), HD)]
        pltpu.make_async_copy(block, block, out_recv.at[head]).wait()
        return carry

    def all_sent(p, carry):
        pz, px = p // ulys, lax.rem(p, ulys)
        for s in range(slots):
            @pl.when(jnp.logical_and(p != me, holds_at(pz, s)))
            def _():
                for t in range(3):
                    copy_to(s, t, pz, px).wait_send()

            @pl.when(jnp.logical_and(p != me, holds_at(z, s)))
            def _():
                out_remote(s, pz, px).wait_send()
        return carry

    lax.fori_loop(0, peers, all_sent, 0)
    lax.fori_loop(0, heads, result_landed, 0)


def exchanged(query_rows, key_rows, value_rows):
    blocks = lax.axis_size("blk")
    ulys = lax.axis_size("uly")
    unused, rows, width = query_rows.shape
    heads = width // HD
    peers = blocks * ulys
    slots = max(head_counts(heads // ulys, blocks))
    total = peers * rows
    return pl.pallas_call(
        functools.partial(exchange_kernel, blocks, ulys, rows, heads),
        out_shape=pltpu.VMEM(query_rows.shape, jnp.bfloat16),
        in_specs=[pl.BlockSpec(memory_space=pl.ANY)] * 3,
        out_specs=pl.BlockSpec(memory_space=pltpu.VMEM),
        scratch_shapes=[
            pltpu.VMEM((slots, total, HD), jnp.bfloat16),
            pltpu.VMEM((slots, total, HD), jnp.bfloat16),
            pltpu.VMEM((slots, total, HD), jnp.bfloat16),
            pltpu.VMEM((total, total), jnp.bfloat16),
            pltpu.VMEM((slots, total, HD), jnp.bfloat16),
            pltpu.SemaphoreType.DMA((slots, 3, peers)),
            pltpu.SemaphoreType.DMA((slots, 3, peers)),
            pltpu.SemaphoreType.DMA((slots, peers)),
            pltpu.SemaphoreType.DMA((heads,)),
            pltpu.SemaphoreType.REGULAR((blocks,)),
        ],
        compiler_params=pltpu.CompilerParams(collective_id=0, has_side_effects=True),
    )(query_rows, key_rows, value_rows)


def local(query_rows, key_rows, value_rows):
    blocks = lax.axis_size("blk")
    ulys = lax.axis_size("uly")
    heads = query_rows.shape[2] // HD
    tokens = query_rows.shape[1] * blocks * ulys
    if heads % ulys == 0 and heads // ulys >= blocks and tokens <= 1024:
        return exchanged(query_rows, key_rows, value_rows)
    return gathered(query_rows, key_rows, value_rows)


def solution(mesh):
    spec = P("cfg", ("groups", "blk", "uly"), None)
    return jax.shard_map(
        local, mesh=mesh, in_specs=(spec, spec, spec), out_specs=spec, check_vma=False
    )
```

```python
import functools
import math

import jax
import jax.numpy as jnp
from jax import lax
from jax.experimental import pallas as pl
from jax.experimental.pallas import tpu as pltpu
from jax.sharding import PartitionSpec as P

HD = 128
MESH = pl.DeviceIdType.MESH


def attend(queries, key_part, value_part):
    query_mat = queries[0, :, 0]
    row_count, head_count, head_size = query_mat.shape
    score_scale = 1.0 / math.sqrt(head_size)
    start_state = (
        jnp.full((head_count, row_count), -1e30, jnp.float32),
        jnp.zeros((head_count, row_count), jnp.float32),
        jnp.zeros((row_count, head_count, head_size), jnp.float32),
    )

    def absorb(state, pieces):
        key_piece = pieces[0][0, :, 0]
        value_piece = pieces[1][0, :, 0]
        scores = (
            jnp.einsum("qhd,khd->hqk", query_mat, key_piece, preferred_element_type=jnp.float32)
            * score_scale
        )
        running, totals, accumulated = state
        new_max = jnp.maximum(running, jnp.max(scores, axis=2))
        weights = jnp.exp(scores - new_max[:, :, None])
        factor = jnp.exp(running - new_max)
        totals = totals * factor + jnp.sum(weights, axis=2)
        probabilities = weights.astype(jnp.bfloat16)
        contrib = jnp.einsum(
            "hqk,khd->qhd", probabilities, value_piece, preferred_element_type=jnp.float32
        )
        accumulated = accumulated * factor.T[:, :, None] + contrib
        return (new_max, totals, accumulated)

    whole_keys, whole_values = (
        lax.all_gather(key_part, "blk", axis=1, tiled=True),
        lax.all_gather(value_part, "blk", axis=1, tiled=True),
    )
    key_count = whole_keys.shape[1]
    block_rows = math.gcd(key_count, 1024)

    def one_block(state, counter):
        offset = counter * block_rows
        key_block = lax.dynamic_slice_in_dim(whole_keys, offset, block_rows, 1)
        value_block = lax.dynamic_slice_in_dim(whole_values, offset, block_rows, 1)
        return (absorb(state, (key_block, value_block)), None)

    result, unused = lax.scan(
        one_block, start_state, jnp.arange(key_count // block_rows, dtype=jnp.int32)
    )
    output = (result[2] / result[1].T[:, :, None]).astype(jnp.bfloat16)
    return output.reshape(1, row_count, 1, head_count, head_size)


def gathered(query_rows, key_rows, value_rows):
    ulysses = lax.axis_size("uly")
    tokens = query_rows.shape[1]
    width = query_rows.shape[2]
    heads_local = width // HD // ulysses

    def moved(array):
        sections = array.reshape(1, tokens, ulysses, heads_local, HD)
        return lax.all_to_all(sections, "uly", split_axis=2, concat_axis=1, tiled=True)

    mixed = attend(moved(query_rows), moved(key_rows), moved(value_rows))
    merged = lax.all_to_all(mixed, "uly", split_axis=1, concat_axis=2, tiled=True)
    return merged.reshape(1, tokens, width)


def head_counts(heads_column, blocks):
    counts = [heads_column // blocks] * blocks
    by_middle = sorted(range(blocks), key=lambda z: (abs(2 * z - (blocks - 1)), z))
    for z in by_middle[: heads_column % blocks]:
        counts[z] += 1
    return counts


def exchange_kernel(
    blocks, ulys, rows, heads, q_ref, k_ref, v_ref, o_ref,
    qb, kb, vb, pb, ob, in_send, in_recv, out_send, out_recv, row_in,
):
    peers = blocks * ulys
    column = heads // ulys
    counts = head_counts(column, blocks)
    starts = [sum(counts[:z]) for z in range(blocks)]
    slots = max(counts)
    z = lax.axis_index("blk")
    x = lax.axis_index("uly")
    me = z * ulys + x
    sources = (q_ref, k_ref, v_ref)
    buffers = (qb, kb, vb)
    fold = (1.0 / math.sqrt(HD)) * math.log2(math.e)
    chunk_rows = ulys * rows

    def first_of(pz):
        first = jnp.int32(0)
        for i in range(blocks):
            first = first + jnp.where(pz > i, counts[i], 0)
        return first

    def holds_at(pz, s):
        has = pz < 0
        for i in range(blocks):
            if counts[i] > s:
                has = jnp.logical_or(has, pz == i)
        return has

    my_head = x * column + first_of(z)
    my_rows = pl.ds(pl.multiple_of(me * rows, rows), rows)
    turn = jnp.where(z < blocks // 2, blocks // 2, 0)

    def piece(t, head):
        return sources[t].at[0, :, pl.ds(pl.multiple_of(head * HD, HD), HD)]

    def copy_to(s, t, pz, px):
        return pltpu.make_async_remote_copy(
            src_ref=piece(t, px * column + first_of(pz) + s),
            dst_ref=buffers[t].at[s, my_rows],
            send_sem=in_send.at[s, t, pz * ulys + px],
            recv_sem=in_recv.at[s, t, me],
            device_id={"blk": pz, "uly": px},
            device_id_type=MESH,
        )

    def send(s, pz, px):
        for t in range(3):
            copy_to(s, t, pz, px).start()

    def token(row, to):
        pl.semaphore_signal(
            row_in.at[row], inc=1, device_id={"blk": to, "uly": x}, device_id_type=MESH
        )

    toward = jnp.where(z < blocks // 2, 1, -1)

    def inside(pz):
        return jnp.logical_and(pz >= 0, pz < blocks)

    paced = holds_at(z, slots - 1)

    def send_inputs():
        def adjacent(side):
            pz = z + side

            @pl.when(inside(pz))
            def _():
                token(z, pz)
                send(0, pz, x)

        adjacent(toward)
        adjacent(-toward)
        for d in range(1, ulys):
            send(0, z, lax.rem(x + d, ulys))

        def further(d, side):
            pz = z + side * d
            onward = z - side

            @pl.when(inside(pz))
            def _():
                pl.semaphore_wait(row_in.at[pz], 1)
                pl.when(inside(onward))(lambda: token(pz, onward))
                for e in range(1, ulys):
                    send(0, pz, lax.rem(x + e, ulys))
                if d > 1:
                    send(0, pz, x)

        for d in range(1, blocks):
            further(d, toward)
            further(d, -toward)
        pl.when(jnp.logical_not(paced))(send_rest)

    def send_rest():
        for s in range(1, slots):
            for i in range(blocks):
                pz = lax.rem(turn + i, blocks)
                for e in range(ulys):
                    px = lax.rem(x + e, ulys)
                    other = jnp.logical_or(pz != z, px != x)
                    pl.when(jnp.logical_and(holds_at(pz, s), other))(
                        functools.partial(send, s, pz, px)
                    )

    barrier = pltpu.get_barrier_semaphore()

    def greet(pz, px):
        pl.semaphore_signal(
            barrier, inc=1, device_id={"blk": pz, "uly": px}, device_id_type=MESH
        )

    pl.when(z > 0)(lambda: greet(z - 1, x))
    pl.when(z < blocks - 1)(lambda: greet(z + 1, x))
    for d in range(1, ulys):
        greet(z, lax.rem(x + d, ulys))
    def own(s):
        for t in range(3):
            pltpu.make_async_copy(
                piece(t, my_head + s), buffers[t].at[s, my_rows], in_recv.at[s, t, me]
            ).start()

    for s in range(slots):
        pl.when(holds_at(z, s))(functools.partial(own, s))
    greeted = (ulys - 1) + jnp.where(z > 0, 1, 0) + jnp.where(z < blocks - 1, 1, 0)
    pl.semaphore_wait(barrier, greeted)

    send_inputs()

    def landed(s, t):
        def one(p, carry):
            block = buffers[t].at[s, pl.ds(pl.multiple_of(p * rows, rows), rows)]
            pltpu.make_async_copy(block, block, in_recv.at[s, t, p]).wait()
            return carry

        lax.fori_loop(0, peers, one, 0)

    def out_copy(s, c, px):
        head = pl.multiple_of((my_head + s) * HD, HD)
        begin = pl.multiple_of((c * ulys + px) * rows, rows)
        return ob.at[s, pl.ds(begin, rows)], o_ref.at[0, :, pl.ds(head, HD)]

    def out_remote(s, c, px):
        src, dst = out_copy(s, c, px)
        return pltpu.make_async_remote_copy(
            src_ref=src, dst_ref=dst,
            send_sem=out_send.at[s, c * ulys + px],
            recv_sem=out_recv.at[my_head + s],
            device_id={"blk": c, "uly": px}, device_id_type=MESH,
        )

    def out_local(s, c, px):
        src, dst = out_copy(s, c, px)
        return pltpu.make_async_copy(src, dst, out_recv.at[my_head + s])

    late = jnp.logical_and(lax.axis_index("cfg") == 1, holds_at(z, slots - 1))

    def send_output(s, c):
        for px in range(ulys):
            mine = jnp.logical_and(c == z, x == px)

            @pl.when(mine)
            def _():
                out_local(s, c, px).start()

            @pl.when(jnp.logical_not(mine))
            def _():
                out_remote(s, c, px).start()

    def send_late():
        for s in range(slots - 1):
            for i in range((blocks + 1) // 2):
                send_output(s, jnp.where(z < blocks // 2, blocks - 1 - i, i))

    def one_slot(s):
        landed(s, 0)
        if s == 0:
            pl.when(paced)(send_rest)
        landed(s, 1)
        totals = []
        for i in range(blocks):
            c = jnp.where(z < blocks // 2, blocks - 1 - i, i)
            span = pl.ds(pl.multiple_of(c * chunk_rows, chunk_rows), chunk_rows)
            scores = lax.dot_general(
                qb[s, span, :], kb[s], (((1,), (1,)), ((), ())),
                preferred_element_type=jnp.float32,
            )
            top = jnp.max(scores, axis=1, keepdims=True)
            weights = jnp.exp2((scores - top) * fold)
            totals.append(jnp.sum(weights, axis=1, keepdims=True))
            pb[span, :] = weights.astype(jnp.bfloat16)
        landed(s, 2)
        if s > 0 and s == slots - 1:
            pl.when(late)(send_late)
        for i in range(blocks):
            c = jnp.where(z < blocks // 2, blocks - 1 - i, i)
            span = pl.ds(pl.multiple_of(c * chunk_rows, chunk_rows), chunk_rows)
            mixed = jnp.dot(pb[span, :], vb[s], preferred_element_type=jnp.float32)
            ob[s, span, :] = (mixed / totals[i]).astype(jnp.bfloat16)
            if s < slots - 1 and 2 * i < blocks:
                pl.when(jnp.logical_not(late))(functools.partial(send_output, s, c))
            else:
                send_output(s, c)

    for s in range(slots):
        if min(counts) > s:
            one_slot(s)
        else:
            pl.when(holds_at(z, s))(functools.partial(one_slot, s))

    def result_landed(head, carry):
        block = o_ref.at[0, :, pl.ds(pl.multiple_of(head * HD, HD), HD)]
        pltpu.make_async_copy(block, block, out_recv.at[head]).wait()
        return carry

    def all_sent(p, carry):
        pz, px = p // ulys, lax.rem(p, ulys)
        for s in range(slots):
            @pl.when(jnp.logical_and(p != me, holds_at(pz, s)))
            def _():
                for t in range(3):
                    copy_to(s, t, pz, px).wait_send()

            @pl.when(jnp.logical_and(p != me, holds_at(z, s)))
            def _():
                out_remote(s, pz, px).wait_send()
        return carry

    lax.fori_loop(0, peers, all_sent, 0)
    lax.fori_loop(0, heads, result_landed, 0)


def exchanged(query_rows, key_rows, value_rows):
    blocks = lax.axis_size("blk")
    ulys = lax.axis_size("uly")
    unused, rows, width = query_rows.shape
    heads = width // HD
    peers = blocks * ulys
    slots = max(head_counts(heads // ulys, blocks))
    total = peers * rows
    return pl.pallas_call(
        functools.partial(exchange_kernel, blocks, ulys, rows, heads),
        out_shape=pltpu.VMEM(query_rows.shape, jnp.bfloat16),
        in_specs=[pl.BlockSpec(memory_space=pl.ANY)] * 3,
        out_specs=pl.BlockSpec(memory_space=pltpu.VMEM),
        scratch_shapes=[
            pltpu.VMEM((slots, total, HD), jnp.bfloat16),
            pltpu.VMEM((slots, total, HD), jnp.bfloat16),
            pltpu.VMEM((slots, total, HD), jnp.bfloat16),
            pltpu.VMEM((total, total), jnp.bfloat16),
            pltpu.VMEM((slots, total, HD), jnp.bfloat16),
            pltpu.SemaphoreType.DMA((slots, 3, peers)),
            pltpu.SemaphoreType.DMA((slots, 3, peers)),
            pltpu.SemaphoreType.DMA((slots, peers)),
            pltpu.SemaphoreType.DMA((heads,)),
            pltpu.SemaphoreType.REGULAR((blocks,)),
        ],
        compiler_params=pltpu.CompilerParams(collective_id=0, has_side_effects=True),
    )(query_rows, key_rows, value_rows)


def local(query_rows, key_rows, value_rows):
    blocks = lax.axis_size("blk")
    ulys = lax.axis_size("uly")
    heads = query_rows.shape[2] // HD
    tokens = query_rows.shape[1] * blocks * ulys
    if heads % ulys == 0 and heads // ulys >= blocks and tokens <= 1024:
        return exchanged(query_rows, key_rows, value_rows)
    return gathered(query_rows, key_rows, value_rows)


def solution(mesh):
    spec = P("cfg", ("groups", "blk", "uly"), None)
    return jax.shard_map(
        local, mesh=mesh, in_specs=(spec, spec, spec), out_specs=spec, check_vma=False
    )
```
